256 devices in a mesh: gz: 64 (over z, y, x_hi), gy: 4 (over x_lo, core).
Axes of the slice: x: 4 (x_hi: 2, x_lo: 2; x = x_hi * 2 + x_lo), y: 4, z: 8, core: 2. Of those that a mesh axis runs over, the one named last changes fastest.
Arguments:
- test_vectors: float32 [4, 256, 384, 256], P(None, 'gz', 'gy'), may hold values from -18 to 18
- conductivity: float32 [256, 384, 256], P('gz', 'gy'), may hold values from 0.1 to 10
Outputs:
- prolongator: float32 [4, 256, 384, 256], P(None, 'gz', 'gy')
- coarse_factors: float32 [10, 64, 96, 64], P(None, 'gz', 'gy')
The draws below stay inside these ranges and needn't reach their ends.
All inputs are finite; a program needn't handle non-finite values.
Results may differ from the reference program's by a relative error of at most 0.0003.
Values sent between devices are 32-bit elements; how exact they have to be, the bound alone decides.
A program may use at most 64 MiB of HBM per device.

```python
import math
import jax
import jax.numpy as jnp
from jax import lax

CZ = 4
CY = 96
NX = 256
NZ = 256
NY = 384


def draw_test_vectors(key, part):
    first_key = jax.random.fold_in(jax.random.fold_in(key, 11), 0)
    third_key = jax.random.fold_in(jax.random.fold_in(key, 11), 2)
    fourth_key = jax.random.fold_in(jax.random.fold_in(key, 11), 3)
    envelope_key = jax.random.fold_in(key, 29)
    z_ramp = 1.0 + 2.0 * jnp.arange(NZ, dtype=jnp.float32) / NZ
    z_ramp = z_ramp[None, :, None, None]
    ordering = jax.random.permutation(third_key, 4)
    levels = jnp.array([0.1, 0.3, 0.6, 1.0], jnp.float32)
    amplitude = levels[ordering] * jax.random.uniform(fourth_key, (4,), jnp.float32, 0.8, 1.0)
    amplitude = amplitude[:, None, None, None]
    log_env = jax.random.uniform(envelope_key, (4, NZ // CZ, NY // CY), jnp.float32, -2.302585, 0.0)
    envelope = jnp.exp(log_env)
    envelope = jnp.repeat(jnp.repeat(envelope, CZ, axis=1), CY, axis=2)[:, :, :, None]
    values = jnp.clip(jax.random.normal(first_key, (4, NZ, NY, NX), jnp.float32), -6.0, 6.0) * z_ramp * amplitude * envelope
    return values.astype(jnp.float32)


def shard_levels(own_key, shape, cuts, low, largest):
    factor_of = 1.0
    for axis_at, shards_of in cuts:
        draws = jax.random.uniform(jax.random.fold_in(jax.random.fold_in(own_key, 6), axis_at), (shards_of,), jnp.float32, low / len(cuts), largest / len(cuts))
        factor_of = factor_of * jnp.repeat(jnp.exp(draws), shape[axis_at] // shards_of).reshape((-1,) + (1,) * (len(shape) - 1 - axis_at))
    return factor_of


def setup_inputs(seed: int = 0) -> dict:
    arg_keys = jax.random.split(jax.random.key(seed), 3)
    test_vectors = draw_test_vectors(jax.random.fold_in(arg_keys[2], 71), 0)
    conductivity = jnp.clip(jnp.exp(math.log(10.0) - 4.6051702 * jax.random.uniform(arg_keys[1], (NZ, NY, NX), jnp.float32) ** shard_levels(arg_keys[1], (NZ, NY, NX), ((0, 64), (1, 4)), -0.2, 0.2)), 0.1, 10.0)
    return dict(test_vectors=test_vectors, conductivity=conductivity)


RELAX_WEIGHT = 2.0 / 3.0
PAIR_LIST = ((0, 0), (0, 1), (0, 2), (0, 3), (1, 1), (1, 2), (1, 3), (2, 2), (2, 3), (3, 3))

def sweep(values_ext, coef_ext):
    center_coef = coef_ext[1:-1, 1:-1]
    center_vals = values_ext[:, 1:-1, 1:-1]
    neighbours = [(coef_ext[2:, 1:-1], values_ext[:, 2:, 1:-1]), (coef_ext[:-2, 1:-1], values_ext[:, :-2, 1:-1]), (coef_ext[1:-1, 2:], values_ext[:, 1:-1, 2:]), (coef_ext[1:-1, :-2], values_ext[:, 1:-1, :-2]), (jnp.roll(center_coef, -1, axis=-1), jnp.roll(center_vals, -1, axis=-1)), (jnp.roll(center_coef, 1, axis=-1), jnp.roll(center_vals, 1, axis=-1))]
    diagonal = jnp.zeros_like(center_coef)
    fluxes = jnp.zeros_like(center_vals)
    for next_coef, next_vals in neighbours:
        weight = 2.0 * center_coef * next_coef / (center_coef + next_coef)
        diagonal = diagonal + weight
        fluxes = fluxes + weight * (center_vals - next_vals)
    return center_vals - RELAX_WEIGHT * fluxes / diagonal

def block_table(across):
    cells = jnp.arange(across) // 4
    return (cells[:, None] == jnp.arange(across // 4)[None, :]).astype(jnp.float32)

def pair_products(fields):
    return jnp.stack([fields[left_idx] * fields[right_idx] for left_idx, right_idx in PAIR_LIST])

def block_sums(values):
    number, layers, height, across = values.shape
    folded = values.reshape(number, layers // 4, 4, height // 4, 4, across).sum(axis=(2, 4))
    flat = jnp.dot(folded.reshape(-1, across), block_table(across), precision=lax.Precision.HIGHEST)
    return flat.reshape(number, layers // 4, height // 4, across // 4)

def spread_blocks(values, across):
    number, layers, height, blocks_x = values.shape
    flat = jnp.dot(values.reshape(-1, blocks_x), block_table(across).T, precision=lax.Precision.HIGHEST)
    spread = flat.reshape(number, layers, height, across)
    spread = jnp.repeat(spread, 4, axis=1)
    return jnp.repeat(spread, 4, axis=2)

def factor(blocks, grams):
    matrix = [[None] * 4 for _ in range(4)]
    for position, pair in enumerate(PAIR_LIST):
        matrix[pair[0]][pair[1]] = grams[position]
    trace = matrix[0][0] + matrix[1][1] + matrix[2][2] + matrix[3][3]
    ridge = 0.64 * (trace / 256.0 + 1e-06)
    upper = [[None] * 4 for _ in range(4)]
    for row_index in range(4):
        for col_index in range(row_index, 4):
            accum = matrix[row_index][col_index]
            if row_index == col_index:
                accum = accum + ridge
            for inner_index in range(row_index):
                accum = accum - upper[inner_index][row_index] * upper[inner_index][col_index]
            if row_index == col_index:
                upper[row_index][row_index] = jnp.sqrt(accum)
            else:
                upper[row_index][col_index] = accum / upper[row_index][row_index]
    listed = jnp.stack([upper[pair[0]][pair[1]] for pair in PAIR_LIST])
    inverse_list = jnp.stack([1.0 / upper[pair[0]][pair[1]] if pair[0] == pair[1] else upper[pair[0]][pair[1]] for pair in PAIR_LIST])
    spread = spread_blocks(inverse_list, blocks.shape[3])
    lookup = {}
    for position, pair in enumerate(PAIR_LIST):
        lookup[pair] = spread[position]
    columns = []
    for col_index in range(4):
        accum = blocks[col_index]
        for inner_index in range(col_index):
            accum = accum - lookup[inner_index, col_index] * columns[inner_index]
        columns.append(accum * lookup[col_index, col_index])
    return (jnp.stack(columns), listed)

def reference(test_vectors, conductivity):
    coef_pad = jnp.pad(conductivity, ((1, 1), (1, 1), (0, 0)), mode='wrap')
    widths = ((0, 0), (1, 1), (1, 1), (0, 0))
    first = sweep(jnp.pad(test_vectors, widths, mode='wrap'), coef_pad)
    relaxed = sweep(jnp.pad(first, widths, mode='wrap'), coef_pad)
    totals = lax.optimization_barrier(jnp.sum(relaxed * relaxed, axis=(1, 2, 3)))
    scales = lax.rsqrt(totals / (NZ * NY * NX) + 1e-06)
    normalized = relaxed * scales[:, None, None, None]
    rolled = jnp.roll(normalized, (-2, -2, -2), axis=(1, 2, 3))
    slabs = jnp.moveaxis(rolled.reshape(4, NZ // 4, 4, NY, NX), 1, 0)

    def one_slab(slab):
        return factor(slab, block_sums(pair_products(slab)))
    prolong, listed = lax.map(one_slab, slabs)
    prolong = jnp.moveaxis(prolong, 0, 1).reshape(4, NZ, NY, NX)
    prolong = jnp.roll(prolong, (2, 2, 2), axis=(1, 2, 3))
    factors = jnp.moveaxis(listed[:, :, 0], 0, 1)
    return (prolong, factors)
```

```python
import functools

import jax
import jax.numpy as jnp
from jax import lax
from jax.experimental import pallas as pl
from jax.experimental.pallas import tpu as pltpu
from jax.sharding import PartitionSpec as P

MESH = pl.DeviceIdType.MESH
F32 = jnp.float32
KEEP = 1.0 / 3.0
STEP = 2.0 / 3.0
PAIRS = ((0, 0), (0, 1), (0, 2), (0, 3), (1, 1), (1, 2), (1, 3), (2, 2), (2, 3), (3, 3))
AT = {pair: i for i, pair in enumerate(PAIRS)}
ROWS = 96
ACROSS = 256
PAD = 8
TILES = ROWS // 8
CHUNK_TILES = 3
CHUNKS = TILES // CHUNK_TILES
CHUNK_ROWS = CHUNK_TILES * 8
ORDER = (0, 3, 1, 2)
N_GZ = 64
N_GY = 4
CELLS = 256 * 384 * 256


def device(z, y, x_hi, x_lo, core):
    return (z * 8 + y * 2 + x_hi, x_lo * 2 + core)


def sum_partners():
    gz, gy = lax.axis_index("gz"), lax.axis_index("gy")
    z, y, x_hi = gz // 8, lax.rem(gz, 8) // 2, lax.rem(gz, 2)
    x_lo, core = gy // 2, lax.rem(gy, 2)
    chip = [device(z, y, x_hi, x_lo, 1 - core)]
    plane = [
        device(z, lax.rem(y + dy, 4), lax.rem(x_hi + dh, 2), lax.rem(x_lo + dl, 2), core)
        for dy in range(4)
        for dh in range(2)
        for dl in range(2)
        if dy or dh or dl
    ]
    column = [device(lax.rem(z + dz, 8), y, x_hi, x_lo, core) for dz in range(1, 8)]
    return chip, plane, column


SUM_SIZES = (1, 15, 7)
SUM_BASE = (0, 1, 16)


def kernel(
    tv_hbm, k_hbm, out_hbm, fac_ref,
    tv, kc, tz, kz, f, fz, wn, r, prod, gsum, mine, zrecv, full, spread,
    ysend, yrecv, fysend, fyrecv, esend, erecv, sum_send, sum_recv,
    load_sem, out_sem, az_send, az_recv, akz_send, akz_recv, bz_send, bz_recv,
    ay_send, ay_recv, by_send, by_recv, gz_send, gz_recv, ey_send, ey_recv,
    s_send, s_recv,
):
    gz, gy = lax.axis_index("gz"), lax.axis_index("gy")
    z_dev = (
        (lax.rem(gz + N_GZ - 1, N_GZ), gy),
        (lax.rem(gz + 1, N_GZ), gy),
    )
    y_dev = (
        (gz, lax.rem(gy + N_GY - 1, N_GY)),
        (gz, lax.rem(gy + 1, N_GY)),
    )
    partners = sum_partners()

    def remote(src, dst, send_sem, recv_sem, to):
        return pltpu.make_async_remote_copy(
            src_ref=src, dst_ref=dst, send_sem=send_sem, recv_sem=recv_sem,
            device_id=to, device_id_type=MESH,
        )

    loads = [
        pltpu.make_async_copy(tv_hbm, tv.at[:, :, pl.ds(PAD, ROWS), :], load_sem.at[0]),
        pltpu.make_async_copy(k_hbm, kc.at[:, pl.ds(PAD, ROWS), :], load_sem.at[1]),
    ]
    for copy in loads:
        copy.start()

    barrier = pltpu.get_barrier_semaphore()
    greeted = list(z_dev) + list(y_dev) + [d for group in partners for d in group]
    for to in greeted:
        pl.semaphore_signal(barrier, inc=1, device_id=to, device_id_type=MESH)

    for copy in loads:
        copy.wait()
    for side, row in ((0, PAD), (1, PAD + ROWS - 1)):
        for p in range(4):
            for v in range(4):
                ysend[side, pl.ds(v * 4 + p, 1), :] = tv[v, p, pl.ds(row, 1), :]
            ysend[side, pl.ds(16 + p, 1), :] = kc[p, pl.ds(row, 1), :]
    for field in range(20):
        for side in range(2):
            prod[field, side, pl.ds(ROWS, 8), :] = jnp.zeros((8, 128), F32)
        gsum[field, pl.ds(24, 8), :] = jnp.zeros((8, ACROSS), F32)

    pl.semaphore_wait(barrier, len(greeted))

    face = (0, 3)
    az, akz = {}, {}
    for c in ORDER:
        rows = pl.ds(c * CHUNK_ROWS, CHUNK_ROWS)
        for side in range(2):
            az[c, side] = remote(
                tv_hbm.at[:, face[side], rows, :], tz.at[1 - side, :, rows, :],
                az_send.at[side, c], az_recv.at[1 - side, c], z_dev[side],
            )
            akz[c, side] = remote(
                k_hbm.at[face[side], rows, :], kz.at[1 - side, rows, :],
                akz_send.at[side, c], akz_recv.at[1 - side, c], z_dev[side],
            )
            akz[c, side].start()
            az[c, side].start()
        if c == ORDER[0]:
            ay = [
                remote(ysend.at[side], yrecv.at[1 - side], ay_send.at[side],
                       ay_recv.at[1 - side], y_dev[side])
                for side in range(2)
            ]
            for copy in ay:
                copy.start()

    for copy in ay:
        copy.wait()
    for side, row in ((0, PAD - 1), (1, PAD + ROWS)):
        for p in range(4):
            for v in range(4):
                tv[v, p, pl.ds(row, 1), :] = yrecv[side, pl.ds(v * 4 + p, 1), :]
            kc[p, pl.ds(row, 1), :] = yrecv[side, pl.ds(16 + p, 1), :]

    def left(x):
        return pltpu.roll(x, 1, 1)

    def right(x):
        return pltpu.roll(x, ACROSS - 1, 1)

    def weights(t, p):
        at = t * 8
        here = kc[p, pl.ds(at + PAD, 8), :]
        near = (
            kc[p + 1, pl.ds(at + PAD, 8), :] if p < 3 else kz[1, pl.ds(at, 8), :],
            kc[p - 1, pl.ds(at + PAD, 8), :] if p > 0 else kz[0, pl.ds(at, 8), :],
            kc[p, pl.ds(at + PAD + 1, 8), :],
            kc[p, pl.ds(at + PAD - 1, 8), :],
            right(here),
            left(here),
        )
        parts = [n / (here + n) for n in near]
        total = ((parts[0] + parts[1]) + (parts[2] + parts[3])) + (parts[4] + parts[5])
        norm = STEP / total
        for i in range(6):
            wn[i, p, pl.ds(at, 8), :] = parts[i] * norm

    def relax(t, p, src, halo):
        at = t * 8
        w = [wn[i, p, pl.ds(at, 8), :] for i in range(6)]
        result = []
        for v in range(4):
            here = src[v, p, pl.ds(at + PAD, 8), :]
            up = src[v, p + 1, pl.ds(at + PAD, 8), :] if p < 3 else halo[1, v, pl.ds(at, 8), :]
            down = src[v, p - 1, pl.ds(at + PAD, 8), :] if p > 0 else halo[0, v, pl.ds(at, 8), :]
            ahead = src[v, p, pl.ds(at + PAD + 1, 8), :]
            behind = src[v, p, pl.ds(at + PAD - 1, 8), :]
            total = (w[0] * up + w[1] * down) + (w[2] * ahead + w[3] * behind)
            total = total + (w[4] * right(here) + w[5] * left(here))
            result.append(here * KEEP + total)
        return result

    def first_tile(t, p):
        for v, value in enumerate(relax(t, p, tv, tz)):
            f[v, p, pl.ds(t * 8 + PAD, 8), :] = value

    def second_tile(t, p):
        for v, value in enumerate(relax(t, p, f, fz)):
            r[v, p, pl.ds(t * 8, 8), :] = value

    for t in range(TILES):
        for p in (1, 2):
            weights(t, p)
            first_tile(t, p)

    bz = {}
    done = []
    for c in ORDER:
        rows = pl.ds(c * CHUNK_ROWS, CHUNK_ROWS)
        rows_in = pl.ds(c * CHUNK_ROWS + PAD, CHUNK_ROWS)
        for side in range(2):
            akz[c, side].wait()
            az[c, side].wait()
        for t in range(c * CHUNK_TILES, (c + 1) * CHUNK_TILES):
            for p in face:
                weights(t, p)
                first_tile(t, p)
        for side in range(2):
            bz[c, side] = remote(
                f.at[:, face[side], rows_in, :], fz.at[1 - side, :, rows, :],
                bz_send.at[side, c], bz_recv.at[1 - side, c], z_dev[side],
            )
            bz[c, side].start()
        done.append(c)
        if len(done) == 2:
            for side, row in ((0, PAD), (1, PAD + ROWS - 1)):
                for p in range(4):
                    for v in range(4):
                        fysend[side, pl.ds(v * 4 + p, 1), :] = f[v, p, pl.ds(row, 1), :]
            by = [
                remote(fysend.at[side], fyrecv.at[1 - side], by_send.at[side],
                       by_recv.at[1 - side], y_dev[side])
                for side in range(2)
            ]
            for copy in by:
                copy.start()

    for copy in by:
        copy.wait()
    for side, row in ((0, PAD - 1), (1, PAD + ROWS)):
        for p in range(4):
            for v in range(4):
                f[v, p, pl.ds(row, 1), :] = fyrecv[side, pl.ds(v * 4 + p, 1), :]
    for t in range(TILES):
        for p in (1, 2):
            second_tile(t, p)

    squares = [jnp.zeros((8, ACROSS), F32) for _ in range(4)]
    for c in ORDER:
        for side in range(2):
            bz[c, side].wait()
        for t in range(c * CHUNK_TILES, (c + 1) * CHUNK_TILES):
            rows = pl.ds(t * 8, 8)
            for half in range(2):
                second_tile(t, face[half])
                low = [r[v, 2 * half, rows, :] for v in range(4)]
                high = [r[v, 2 * half + 1, rows, :] for v in range(4)]
                for i, (a, b) in enumerate(PAIRS):
                    value = low[a] * low[b] + high[a] * high[b]
                    prod[half * 10 + i, 0, rows, :] = value[:, :128]
                    prod[half * 10 + i, 1, rows, :] = value[:, 128:]
                    if a == b:
                        squares[a] = squares[a] + value

    def exchange(stage):
        sends = []
        for i, to in enumerate(partners[stage]):
            at = SUM_BASE[stage] + i
            copy = remote(sum_send.at[stage], sum_recv.at[at], s_send.at[at], s_recv.at[at], to)
            copy.start()
            sends.append(copy)
        return sends

    def collect(stage, sends):
        total = sum_send[stage]
        for i, copy in enumerate(sends):
            copy.wait()
            total = total + sum_recv[SUM_BASE[stage] + i]
        return total

    for v in range(4):
        both = squares[v][:, :128] + squares[v][:, 128:]
        sum_send[0, pl.ds(v, 1), :] = jnp.sum(both, axis=0, keepdims=True)
    sum_send[0, pl.ds(4, 4), :] = jnp.zeros((4, 128), F32)
    sends = exchange(0)

    for field in range(20):
        for side in range(2):
            own = pl.ds(side * 128, 128)
            parts = [prod[field, side, pl.ds(2 + i, 24, stride=4), :] for i in range(4)]
            gsum[field, pl.ds(0, 24), own] = (parts[0] + parts[1]) + (parts[2] + parts[3])
            gsum[field, pl.ds(24, 1), own] = (
                prod[field, side, pl.ds(0, 1), :] + prod[field, side, pl.ds(1, 1), :]
            )
    cell = lax.rem(lax.broadcasted_iota(jnp.int32, (ACROSS, 128), 0) + ACROSS - 2, ACROSS) // 4
    lane = lax.broadcasted_iota(jnp.int32, (ACROSS, 128), 1)
    pick_low = (cell == lane).astype(F32)
    pick_high = (cell + 64 == lane).astype(F32)
    for half in range(2):
        a = gsum[pl.ds(half * 10, 5), :, :].reshape(160, ACROSS)
        b = gsum[pl.ds(half * 10 + 5, 5), :, :].reshape(160, ACROSS)
        packed = jnp.dot(a, pick_low, precision=lax.Precision.HIGHEST, preferred_element_type=F32)
        packed = packed + jnp.dot(
            b, pick_high, precision=lax.Precision.HIGHEST, preferred_element_type=F32
        )
        mine[half] = packed.reshape(5, 32, 128)
    gz_copies = [
        remote(mine.at[half], zrecv.at[1 - half], gz_send.at[half], gz_recv.at[1 - half], z_dev[half])
        for half in range(2)
    ]
    for copy in gz_copies:
        copy.start()

    sum_send[1] = collect(0, sends)
    sends = exchange(1)
    sum_send[2] = collect(1, sends)
    sends = exchange(2)

    for copy in gz_copies:
        copy.wait()
    for half in range(2):
        total = mine[half] + zrecv[half]
        full[half] = total
        for i in range(5):
            esend[0, pl.ds(half * 5 + i, 1), :] = total[i, 24:25]
            esend[1, pl.ds(half * 5 + i, 1), :] = total[i, 23:24]
    ey = [
        remote(esend.at[side], erecv.at[1 - side], ey_send.at[side], ey_recv.at[1 - side], y_dev[side])
        for side in range(2)
    ]
    for copy in ey:
        copy.start()
    for copy in ey:
        copy.wait()
    for half in range(2):
        for i in range(5):
            n = half * 5 + i
            full[half, i, pl.ds(24, 1), :] = esend[0, pl.ds(n, 1), :] + erecv[0, pl.ds(n, 1), :]
            full[half, i, pl.ds(23, 1), :] = esend[1, pl.ds(n, 1), :] + erecv[1, pl.ds(n, 1), :]

    lanes = lax.broadcasted_iota(jnp.int32, (32, 128), 1)
    is_low = lanes < 64
    gram = [None] * 10
    for i in range(5):
        low, high = full[0, i], full[1, i]
        gram[i] = jnp.where(is_low, low, pltpu.roll(high, 64, 1))
        gram[i + 5] = jnp.where(is_low, pltpu.roll(low, 64, 1), high)

    across = lax.broadcasted_iota(jnp.int32, (128, 2 * ACROSS), 1)
    owner = lax.rem(lax.rem(across, ACROSS) + ACROSS - 2, ACROSS) // 4 + (across // ACROSS) * 64
    expand = (lax.broadcasted_iota(jnp.int32, (128, 2 * ACROSS), 0) == owner).astype(F32)

    totals = jnp.sum(collect(2, sends), axis=1, keepdims=True)
    scale_col = lax.rsqrt(totals / CELLS + 1e-06)
    scale = [jnp.broadcast_to(scale_col[v : v + 1, :], (32, 128)) for v in range(4)]

    m = {pair: gram[i] * (scale[pair[0]] * scale[pair[1]]) for i, pair in enumerate(PAIRS)}
    trace = (m[0, 0] + m[1, 1]) + (m[2, 2] + m[3, 3])
    ridge = 0.64 * (trace / 256.0 + 1e-06)
    upper, inverse = {}, []
    for i in range(4):
        for j in range(i, 4):
            value = m[i, j]
            if i == j:
                value = value + ridge
            for n in range(i):
                value = value - upper[n, i] * upper[n, j]
            if i == j:
                upper[i, i] = jnp.sqrt(value)
                inverse.append(1.0 / upper[i, i])
            else:
                upper[i, j] = value * inverse[i]
    table = []
    for n, (i, j) in enumerate(PAIRS):
        fac_ref[n, 0] = pltpu.roll(upper[i, j], 64, 1)[:24, :64]
        table.append((scale[j] if i == j else upper[i, j]) * inverse[j])
    stacked = jnp.concatenate(table, axis=0)
    wide = jnp.dot(stacked, expand, precision=lax.Precision.HIGHEST, preferred_element_type=F32)
    spread[...] = wide.reshape(10, 32, 2 * ACROSS)

    sub = lax.broadcasted_iota(jnp.int32, (8, ACROSS), 0)
    before, after = sub < 2, sub >= 6
    outs = []
    for c in range(CHUNKS):
        for t in range(c * CHUNK_TILES, (c + 1) * CHUNK_TILES):
            rows = pl.ds(t * 8, 8)
            for half in range(2):
                columns = pl.ds(half * ACROSS, ACROSS)
                field = []
                for n in range(10):
                    one = spread[n, pl.ds(24 if t == 0 else 2 * t - 1, 1), columns]
                    two = spread[n, pl.ds(2 * t, 1), columns]
                    three = spread[n, pl.ds(2 * t + 1, 1), columns]
                    field.append(jnp.where(before, one, jnp.where(after, three, two)))
                for p in (2 * half, 2 * half + 1):
                    done_columns = []
                    for j in range(4):
                        value = r[j, p, rows, :] * field[AT[j, j]]
                        for i in range(j):
                            value = value - field[AT[i, j]] * done_columns[i]
                        done_columns.append(value)
                        r[j, p, rows, :] = value
        rows = pl.ds(c * CHUNK_ROWS, CHUNK_ROWS)
        copy = pltpu.make_async_copy(r.at[:, :, rows, :], out_hbm.at[:, :, rows, :], out_sem.at[c])
        copy.start()
        outs.append(copy)
    for copy in outs:
        copy.wait()


def body(test_vectors, conductivity):
    vm = lambda *shape: pltpu.VMEM(shape, F32)
    dma = lambda *shape: pltpu.SemaphoreType.DMA(shape)
    return pl.pallas_call(
        kernel,
        out_shape=(
            jax.ShapeDtypeStruct((4, 4, ROWS, ACROSS), F32),
            jax.ShapeDtypeStruct((10, 1, 24, 64), F32),
        ),
        in_specs=[pl.BlockSpec(memory_space=pl.ANY)] * 2,
        out_specs=(
            pl.BlockSpec(memory_space=pl.ANY),
            pl.BlockSpec(memory_space=pltpu.VMEM),
        ),
        scratch_shapes=[
            vm(4, 4, ROWS + 2 * PAD, ACROSS),
            vm(4, ROWS + 2 * PAD, ACROSS),
            vm(2, 4, ROWS, ACROSS),
            vm(2, ROWS, ACROSS),
            vm(4, 4, ROWS + 2 * PAD, ACROSS),
            vm(2, 4, ROWS, ACROSS),
            vm(6, 4, ROWS, ACROSS),
            vm(4, 4, ROWS, ACROSS),
            vm(20, 2, ROWS + 8, 128),
            vm(20, 32, ACROSS),
            vm(2, 5, 32, 128),
            vm(2, 5, 32, 128),
            vm(2, 5, 32, 128),
            vm(10, 32, 2 * ACROSS),
            vm(2, 24, ACROSS),
            vm(2, 24, ACROSS),
            vm(2, 16, ACROSS),
            vm(2, 16, ACROSS),
            vm(2, 16, 128),
            vm(2, 16, 128),
            vm(3, 8, 128),
            vm(23, 8, 128),
            dma(2), dma(CHUNKS),
            dma(2, CHUNKS), dma(2, CHUNKS), dma(2, CHUNKS), dma(2, CHUNKS),
            dma(2, CHUNKS), dma(2, CHUNKS),
            dma(2), dma(2), dma(2), dma(2), dma(2), dma(2), dma(2), dma(2),
            dma(23), dma(23),
        ],
        compiler_params=pltpu.CompilerParams(collective_id=0, has_side_effects=True),
        name="bootstrap",
    )(test_vectors, conductivity)


def solution(mesh):
    return jax.shard_map(
        body,
        mesh=mesh,
        in_specs=(P(None, "gz", "gy", None), P("gz", "gy", None)),
        out_specs=(P(None, "gz", "gy", None), P(None, "gz", "gy", None)),
        check_vma=False,
    )
```

```python
import functools

import jax
import jax.numpy as jnp
from jax import lax
from jax.experimental import pallas as pl
from jax.experimental.pallas import tpu as pltpu
from jax.sharding import PartitionSpec as P

MESH = pl.DeviceIdType.MESH
F32 = jnp.float32
KEEP = 1.0 / 3.0
STEP = 2.0 / 3.0
PAIRS = ((0, 0), (0, 1), (0, 2), (0, 3), (1, 1), (1, 2), (1, 3), (2, 2), (2, 3), (3, 3))
AT = {pair: i for i, pair in enumerate(PAIRS)}
BF16 = jnp.bfloat16
ROWS = 96
ACROSS = 256
PAD = 8
TILES = ROWS // 8
CHUNKS = ((0, 3), (8, 4), (3, 3), (6, 2))
EARLY = 88
LATE = 40
N_GZ = 64
N_GY = 4
CELLS = 256 * 384 * 256


def device(z, y, x_hi, x_lo, core):
    return (z * 8 + y * 2 + x_hi, x_lo * 2 + core)


def sum_partners():
    gz, gy = lax.axis_index("gz"), lax.axis_index("gy")
    z, y, x_hi = gz // 8, lax.rem(gz, 8) // 2, lax.rem(gz, 2)
    x_lo, core = gy // 2, lax.rem(gy, 2)
    chip = [device(z, y, x_hi, x_lo, 1 - core)]
    plane = [
        device(z, lax.rem(y + dy, 4), lax.rem(x_hi + dh, 2), lax.rem(x_lo + dl, 2), core)
        for dy in range(4)
        for dh in range(2)
        for dl in range(2)
        if dy or dh or dl
    ]
    column = [device(lax.rem(z + dz, 8), y, x_hi, x_lo, core) for dz in range(1, 8)]
    return chip, column, plane


SUM_BASE = (0, 1, 8)


def spans():
    return [(c, tile * 8, tiles * 8) for c, (tile, tiles) in enumerate(CHUNKS)]


def split_dot(x, table):
    high = x.astype(BF16)
    rest = x - high.astype(F32)
    middle = rest.astype(BF16)
    low = (rest - middle.astype(F32)).astype(BF16)
    one = jnp.dot(low, table, preferred_element_type=F32)
    two = jnp.dot(middle, table, preferred_element_type=F32)
    return (one + two) + jnp.dot(high, table, preferred_element_type=F32)


def kernel(
    tv_hbm, k_hbm, r, gram_early, gram_late, total_ref,
    tv, kc, tz, kz, f, fz, wn, prod, sum_early, sum_late,
    mine_early, mine_late, from_early, from_late,
    ysend, yrecv, fysend, fyrecv, esend, erecv, sum_send, sum_recv,
    load_sem, az_send, az_recv, akz_send, akz_recv, bz_send, bz_recv,
    ay_send, ay_recv, by_send, by_recv, ge_send, ge_recv, gl_send, gl_recv,
    ey_send, ey_recv, s_send, s_recv,
):
    gz, gy = lax.axis_index("gz"), lax.axis_index("gy")
    z_dev = (
        (lax.rem(gz + N_GZ - 1, N_GZ), gy),
        (lax.rem(gz + 1, N_GZ), gy),
    )
    y_dev = (
        (gz, lax.rem(gy + N_GY - 1, N_GY)),
        (gz, lax.rem(gy + 1, N_GY)),
    )
    partners = sum_partners()

    def remote(src, dst, send_sem, recv_sem, to):
        return pltpu.make_async_remote_copy(
            src_ref=src, dst_ref=dst, send_sem=send_sem, recv_sem=recv_sem,
            device_id=to, device_id_type=MESH,
        )

    loads = [
        pltpu.make_async_copy(tv_hbm, tv.at[:, :, pl.ds(PAD, ROWS), :], load_sem.at[0]),
        pltpu.make_async_copy(k_hbm, kc.at[:, pl.ds(PAD, ROWS), :], load_sem.at[1]),
    ]
    for copy in loads:
        copy.start()

    barrier = pltpu.get_barrier_semaphore()
    greeted = list(z_dev) + list(y_dev) + [d for group in partners for d in group]
    for to in greeted:
        pl.semaphore_signal(barrier, inc=1, device_id=to, device_id_type=MESH)

    for copy in loads:
        copy.wait()
    for side, row in ((0, PAD), (1, PAD + ROWS - 1)):
        for p in range(4):
            for v in range(4):
                ysend[side, pl.ds(v * 4 + p, 1), :] = tv[v, p, pl.ds(row, 1), :]
            ysend[side, pl.ds(16 + p, 1), :] = kc[p, pl.ds(row, 1), :]
    for field in range(20):
        for side in range(2):
            prod[field, side, pl.ds(ROWS, 8), :] = jnp.zeros((8, 128), F32)
    for half in range(2):
        for part in range(2):
            sum_early[half, part, pl.ds(80, 8), :] = jnp.zeros((8, ACROSS), F32)

    pl.semaphore_wait(barrier, len(greeted))

    face = (0, 3)
    az, akz = {}, {}
    for c, start, count in spans():
        rows = pl.ds(start, count)
        for side in range(2):
            az[c, side] = remote(
                tv_hbm.at[:, face[side], rows, :], tz.at[1 - side, :, rows, :],
                az_send.at[side, c], az_recv.at[1 - side, c], z_dev[side],
            )
            akz[c, side] = remote(
                k_hbm.at[face[side], rows, :], kz.at[1 - side, rows, :],
                akz_send.at[side, c], akz_recv.at[1 - side, c], z_dev[side],
            )
            akz[c, side].start()
            az[c, side].start()
        if c == 0:
            ay = [
                remote(ysend.at[side], yrecv.at[1 - side], ay_send.at[side],
                       ay_recv.at[1 - side], y_dev[side])
                for side in range(2)
            ]
            for copy in ay:
                copy.start()

    for copy in ay:
        copy.wait()
    for side, row in ((0, PAD - 1), (1, PAD + ROWS)):
        for p in range(4):
            for v in range(4):
                tv[v, p, pl.ds(row, 1), :] = yrecv[side, pl.ds(v * 4 + p, 1), :]
            kc[p, pl.ds(row, 1), :] = yrecv[side, pl.ds(16 + p, 1), :]

    def left(x):
        return pltpu.roll(x, 1, 1)

    def right(x):
        return pltpu.roll(x, ACROSS - 1, 1)

    def weights(t, p):
        at = t * 8
        here = kc[p, pl.ds(at + PAD, 8), :]
        near = (
            kc[p + 1, pl.ds(at + PAD, 8), :] if p < 3 else kz[1, pl.ds(at, 8), :],
            kc[p - 1, pl.ds(at + PAD, 8), :] if p > 0 else kz[0, pl.ds(at, 8), :],
            kc[p, pl.ds(at + PAD + 1, 8), :],
            kc[p, pl.ds(at + PAD - 1, 8), :],
            right(here),
            left(here),
        )
        parts = [n / (here + n) for n in near]
        total = ((parts[0] + parts[1]) + (parts[2] + parts[3])) + (parts[4] + parts[5])
        norm = STEP / total
        for i in range(6):
            wn[i, p, pl.ds(at, 8), :] = parts[i] * norm

    def relax(t, p, src, halo):
        at = t * 8
        w = [wn[i, p, pl.ds(at, 8), :] for i in range(6)]
        result = []
        for v in range(4):
            here = src[v, p, pl.ds(at + PAD, 8), :]
            up = src[v, p + 1, pl.ds(at + PAD, 8), :] if p < 3 else halo[1, v, pl.ds(at, 8), :]
            down = src[v, p - 1, pl.ds(at + PAD, 8), :] if p > 0 else halo[0, v, pl.ds(at, 8), :]
            ahead = src[v, p, pl.ds(at + PAD + 1, 8), :]
            behind = src[v, p, pl.ds(at + PAD - 1, 8), :]
            total = (w[0] * up + w[1] * down) + (w[2] * ahead + w[3] * behind)
            total = total + (w[4] * right(here) + w[5] * left(here))
            result.append(here * KEEP + total)
        return result

    def first_tile(t, p):
        for v, value in enumerate(relax(t, p, tv, tz)):
            f[v, p, pl.ds(t * 8 + PAD, 8), :] = value

    def second_tile(t, p):
        for v, value in enumerate(relax(t, p, f, fz)):
            r[v, p, pl.ds(t * 8, 8), :] = value

    for t in range(TILES):
        for p in (1, 2):
            weights(t, p)
            first_tile(t, p)

    bz = {}
    for c, start, count in spans():
        rows = pl.ds(start, count)
        rows_in = pl.ds(start + PAD, count)
        for side in range(2):
            akz[c, side].wait()
            az[c, side].wait()
        for t in range(start // 8, (start + count) // 8):
            for p in face:
                weights(t, p)
                first_tile(t, p)
        for side in range(2):
            bz[c, side] = remote(
                f.at[:, face[side], rows_in, :], fz.at[1 - side, :, rows, :],
                bz_send.at[side, c], bz_recv.at[1 - side, c], z_dev[side],
            )
            bz[c, side].start()
        if c == 1:
            for side, row in ((0, PAD), (1, PAD + ROWS - 1)):
                for p in range(4):
                    for v in range(4):
                        fysend[side, pl.ds(v * 4 + p, 1), :] = f[v, p, pl.ds(row, 1), :]
            by = [
                remote(fysend.at[side], fyrecv.at[1 - side], by_send.at[side],
                       by_recv.at[1 - side], y_dev[side])
                for side in range(2)
            ]
            for copy in by:
                copy.start()

    for copy in by:
        copy.wait()
    for side, row in ((0, PAD - 1), (1, PAD + ROWS)):
        for p in range(4):
            for v in range(4):
                f[v, p, pl.ds(row, 1), :] = fyrecv[side, pl.ds(v * 4 + p, 1), :]
    for t in range(TILES):
        for p in (1, 2):
            second_tile(t, p)

    def group_sums(field, first_row, into, at):
        for side in range(2):
            parts = [prod[field, side, pl.ds(first_row + i, 8, stride=4), :] for i in range(4)]
            into[field // 10, (field % 10) // 5, pl.ds(at, 8), pl.ds(side * 128, 128)] = (
                (parts[0] + parts[1]) + (parts[2] + parts[3])
            )

    cell = ((lax.broadcasted_iota(jnp.int32, (ACROSS, 128), 0) + (ACROSS - 2)) & (ACROSS - 1)) >> 2
    lane = lax.broadcasted_iota(jnp.int32, (ACROSS, 128), 1)
    pick = [(cell + 64 * part == lane).astype(F32).astype(BF16) for part in range(2)]

    def pack(sums, half):
        return split_dot(sums[half, 0], pick[0]) + split_dot(sums[half, 1], pick[1])

    squares = [jnp.zeros((8, ACROSS), F32) for _ in range(4)]
    for c, start, count in spans():
        if c == len(CHUNKS) - 1:
            for field in range(20):
                n = field % 5
                group_sums(field, 2, sum_early, n * 8)
                group_sums(field, 66, sum_early, 40 + n * 8)
                for side in range(2):
                    sum_early[field // 10, (field % 10) // 5, pl.ds(80 + n, 1), pl.ds(side * 128, 128)] = (
                        prod[field, side, pl.ds(0, 1), :] + prod[field, side, pl.ds(1, 1), :]
                    )
            for half in range(2):
                mine_early[half] = pack(sum_early, half)
            ge = [
                remote(mine_early.at[half], from_early.at[1 - half], ge_send.at[half],
                       ge_recv.at[1 - half], z_dev[half])
                for half in range(2)
            ]
            for copy in ge:
                copy.start()
        for side in range(2):
            bz[c, side].wait()
        for t in range(start // 8, (start + count) // 8):
            rows = pl.ds(t * 8, 8)
            for half in range(2):
                second_tile(t, face[half])
                low = [r[v, 2 * half, rows, :] for v in range(4)]
                high = [r[v, 2 * half + 1, rows, :] for v in range(4)]
                for i, (a, b) in enumerate(PAIRS):
                    value = low[a] * low[b] + high[a] * high[b]
                    prod[half * 10 + i, 0, rows, :] = value[:, :128]
                    prod[half * 10 + i, 1, rows, :] = value[:, 128:]
                    if a == b:
                        squares[a] = squares[a] + value

    def exchange(stage):
        sends = []
        for i, to in enumerate(partners[stage]):
            at = SUM_BASE[stage] + i
            copy = remote(sum_send.at[stage], sum_recv.at[at], s_send.at[at], s_recv.at[at], to)
            copy.start()
            sends.append(copy)
        return sends

    def collect(stage, sends):
        for copy in sends:
            copy.wait()
        total = [sum_send[stage]] + [sum_recv[SUM_BASE[stage] + i] for i in range(len(sends))]
        while len(total) > 1:
            total = [sum(total[i : i + 2][1:], total[i]) for i in range(0, len(total), 2)]
        return total[0]

    stacked = [jnp.sum(q[:, :128] + q[:, 128:], axis=0, keepdims=True) for q in squares]
    stacked = jnp.concatenate(stacked + [jnp.zeros((4, 128), F32)], axis=0)
    stacked = jnp.sum(stacked, axis=1, keepdims=True)
    on_diagonal = lax.broadcasted_iota(jnp.int32, (8, 128), 0) == lax.broadcasted_iota(
        jnp.int32, (8, 128), 1
    )
    sum_send[0] = jnp.sum(jnp.where(on_diagonal, stacked, 0.0), axis=0, keepdims=True)
    sends = exchange(0)

    for field in range(20):
        group_sums(field, 34, sum_late, (field % 5) * 8)
    for half in range(2):
        mine_late[half] = pack(sum_late, half)
    gl = [
        remote(mine_late.at[half], from_late.at[1 - half], gl_send.at[half],
               gl_recv.at[1 - half], z_dev[half])
        for half in range(2)
    ]
    for copy in gl:
        copy.start()

    sum_send[1] = collect(0, sends)
    sends = exchange(1)

    for copy in ge:
        copy.wait()
    for half in range(2):
        total = mine_early[half] + from_early[half]
        gram_early[half] = total
        esend[0, half] = total[80:88]
        for i in range(5):
            esend[1, half, pl.ds(i, 1), :] = total[47 + 8 * i : 48 + 8 * i]
        esend[1, half, pl.ds(5, 3), :] = jnp.zeros((3, 128), F32)
    ey = [
        remote(esend.at[side], erecv.at[1 - side], ey_send.at[side], ey_recv.at[1 - side], y_dev[side])
        for side in range(2)
    ]
    for copy in ey:
        copy.start()

    sum_send[2] = collect(1, sends)
    sends = exchange(2)

    for copy in ey:
        copy.wait()
    for half in range(2):
        gram_early[half, pl.ds(80, 8), :] = esend[0, half] + erecv[0, half]
        for i in range(5):
            one = pl.ds(i, 1)
            gram_early[half, pl.ds(47 + 8 * i, 1), :] = esend[1, half, one, :] + erecv[1, half, one, :]
    for copy in gl:
        copy.wait()
    for half in range(2):
        gram_late[half] = mine_late[half] + from_late[half]
    total_ref[...] = jnp.broadcast_to(collect(2, sends), (8, 128))


def finish(
    r, gram_early, gram_late, total_ref, out_hbm, fac_hbm, spread, out, fac, out_sem, fac_sem
):
    across = lax.broadcasted_iota(jnp.int32, (128, 2 * ACROSS), 1)
    owner = (((across + (ACROSS - 2)) & (ACROSS - 1)) >> 2) + ((across >> 8) << 6)
    expand = (lax.broadcasted_iota(jnp.int32, (128, 2 * ACROSS), 0) == owner).astype(F32).astype(BF16)

    is_low = lax.broadcasted_iota(jnp.int32, (32, 128), 1) < 64
    lane = lax.broadcasted_iota(jnp.int32, (1, 128), 1)
    scale_row = lax.rsqrt(total_ref[0:1, :] / CELLS + 1e-06)
    scale = [
        jnp.sum(jnp.where(lane == v, scale_row, 0.0), axis=1, keepdims=True) for v in range(4)
    ]

    def groups(half, i):
        edge = jnp.broadcast_to(gram_early[half, pl.ds(80 + i, 1), :], (8, 128))
        return jnp.concatenate(
            [
                gram_early[half, pl.ds(8 * i, 8), :],
                gram_late[half, pl.ds(8 * i, 8), :],
                gram_early[half, pl.ds(40 + 8 * i, 8), :],
                edge,
            ],
            axis=0,
        )

    gram = [None] * 10
    for i in range(5):
        low, high = groups(0, i), groups(1, i)
        gram[i] = jnp.where(is_low, low, pltpu.roll(high, 64, 1))
        gram[i + 5] = jnp.where(is_low, pltpu.roll(low, 64, 1), high)

    m = {pair: gram[i] * (scale[pair[0]] * scale[pair[1]]) for i, pair in enumerate(PAIRS)}
    trace = (m[0, 0] + m[1, 1]) + (m[2, 2] + m[3, 3])
    ridge = 0.64 * (trace / 256.0 + 1e-06)
    upper, inverse = {}, []
    for i in range(4):
        for j in range(i, 4):
            value = m[i, j]
            if i == j:
                value = value + ridge
            for n in range(i):
                value = value - upper[n, i] * upper[n, j]
            if i == j:
                upper[i, i] = jnp.sqrt(value)
                inverse.append(1.0 / upper[i, i])
            else:
                upper[i, j] = value * inverse[i]
    table = [(scale[j] if i == j else upper[i, j]) * inverse[j] for i, j in PAIRS]
    wide = split_dot(jnp.concatenate(table, axis=0), expand)
    spread[...] = wide.reshape(10, 32, 2 * ACROSS)
    for n, pair in enumerate(PAIRS):
        fac[n, 0] = pltpu.roll(upper[pair], 64, 1)[:24, :64]
    fac_copy = pltpu.make_async_copy(fac, fac_hbm, fac_sem)
    fac_copy.start()

    sub = lax.broadcasted_iota(jnp.int32, (8, ACROSS), 0)
    before, after = sub < 2, sub >= 6
    outs = []
    for c in range(4):
        for t in range(c * 3, c * 3 + 3):
            rows = pl.ds(t * 8, 8)
            for half in range(2):
                columns = pl.ds(half * ACROSS, ACROSS)
                field = []
                for n in range(10):
                    one = spread[n, pl.ds(24 if t == 0 else 2 * t - 1, 1), columns]
                    two = spread[n, pl.ds(2 * t, 1), columns]
                    three = spread[n, pl.ds(2 * t + 1, 1), columns]
                    field.append(jnp.where(before, one, jnp.where(after, three, two)))
                for p in (2 * half, 2 * half + 1):
                    done_columns = []
                    for j in range(4):
                        value = r[j, p, rows, :] * field[AT[j, j]]
                        for i in range(j):
                            value = value - field[AT[i, j]] * done_columns[i]
                        done_columns.append(value)
                        out[j, p, rows, :] = value
        rows = pl.ds(c * 24, 24)
        copy = pltpu.make_async_copy(out.at[:, :, rows, :], out_hbm.at[:, :, rows, :], out_sem.at[c])
        copy.start()
        outs.append(copy)
    fac_copy.wait()
    for copy in outs:
        copy.wait()


def body(test_vectors, conductivity):
    vm = lambda *shape: pltpu.VMEM(shape, F32)
    dma = lambda *shape: pltpu.SemaphoreType.DMA(shape)
    shape = lambda *dims: jax.ShapeDtypeStruct(dims, F32)
    in_vmem = pl.BlockSpec(memory_space=pltpu.VMEM)
    anywhere = pl.BlockSpec(memory_space=pl.ANY)
    n = len(CHUNKS)
    padded = ROWS + 2 * PAD
    staged = pl.pallas_call(
        kernel,
        out_shape=(
            shape(4, 4, ROWS, ACROSS),
            shape(2, EARLY, 128),
            shape(2, LATE, 128),
            shape(8, 128),
        ),
        in_specs=[pl.BlockSpec(memory_space=pltpu.HBM)] * 2,
        out_specs=(in_vmem,) * 4,
        scratch_shapes=[
            vm(4, 4, padded, ACROSS),
            vm(4, padded, ACROSS),
            vm(2, 4, ROWS, ACROSS),
            vm(2, ROWS, ACROSS),
            vm(4, 4, padded, ACROSS),
            vm(2, 4, ROWS, ACROSS),
            vm(6, 4, ROWS, ACROSS),
            vm(20, 2, ROWS + 8, 128),
            vm(2, 2, EARLY, ACROSS),
            vm(2, 2, LATE, ACROSS),
            vm(2, EARLY, 128),
            vm(2, LATE, 128),
            vm(2, EARLY, 128),
            vm(2, LATE, 128),
            vm(2, 24, ACROSS),
            vm(2, 24, ACROSS),
            vm(2, 16, ACROSS),
            vm(2, 16, ACROSS),
            vm(2, 2, 8, 128),
            vm(2, 2, 8, 128),
            vm(3, 1, 128),
            vm(23, 1, 128),
            dma(2),
            dma(2, n), dma(2, n), dma(2, n), dma(2, n), dma(2, n), dma(2, n),
            dma(2), dma(2), dma(2), dma(2), dma(2), dma(2), dma(2), dma(2), dma(2), dma(2),
            dma(23), dma(23),
        ],
        compiler_params=pltpu.CompilerParams(
            collective_id=0, has_side_effects=True, vmem_limit_bytes=24 << 20
        ),
        name="relax",
    )(*[pltpu.with_memory_space_constraint(x, pltpu.HBM) for x in (test_vectors, conductivity)])
    return pl.pallas_call(
        finish,
        out_shape=(shape(4, 4, ROWS, ACROSS), shape(10, 1, 24, 64)),
        in_specs=[in_vmem] * 4,
        out_specs=(anywhere, anywhere),
        scratch_shapes=[
            vm(10, 32, 2 * ACROSS),
            vm(4, 4, ROWS, ACROSS),
            vm(10, 1, 24, 64),
            dma(4),
            pltpu.SemaphoreType.DMA,
        ],
        compiler_params=pltpu.CompilerParams(vmem_limit_bytes=16 << 20),
        name="finish",
    )(*staged)


def solution(mesh):
    return jax.shard_map(
        body,
        mesh=mesh,
        in_specs=(P(None, "gz", "gy", None), P("gz", "gy", None)),
        out_specs=(P(None, "gz", "gy", None), P(None, "gz", "gy", None)),
        check_vma=False,
    )
```

```python
import functools

import jax
import jax.numpy as jnp
from jax import lax
from jax.experimental import pallas as pl
from jax.experimental.pallas import tpu as pltpu
from jax.sharding import PartitionSpec as P

MESH = pl.DeviceIdType.MESH
F32 = jnp.float32
KEEP = 1.0 / 3.0
STEP = 2.0 / 3.0
PAIRS = ((0, 0), (0, 1), (0, 2), (0, 3), (1, 1), (1, 2), (1, 3), (2, 2), (2, 3), (3, 3))
AT = {pair: i for i, pair in enumerate(PAIRS)}
BF16 = jnp.bfloat16
ROWS = 96
ACROSS = 256
PAD = 8
TILES = ROWS // 8
CHUNKS = ((0, 3), (8, 4), (3, 3), (6, 2))
EARLY = 88
LATE = 40
N_GZ = 64
N_GY = 4
CELLS = 256 * 384 * 256


def device(z, y, x_hi, x_lo, core):
    return (z * 8 + y * 2 + x_hi, x_lo * 2 + core)


def sum_partners():
    gz, gy = lax.axis_index("gz"), lax.axis_index("gy")
    z, y, x_hi = gz // 8, lax.rem(gz, 8) // 2, lax.rem(gz, 2)
    x_lo, core = gy // 2, lax.rem(gy, 2)
    column = [
        device(lax.rem(z + dz, 8), y, x_hi, x_lo, lax.rem(core + dc, 2))
        for dz in (4, 3, 5, 2, 6, 1, 7, 0)
        for dc in (1, 0)
        if dz or dc
    ]
    plane = [
        device(z, lax.rem(y + dy, 4), lax.rem(x_hi + dh, 2), lax.rem(x_lo + dl, 2), core)
        for dy in (2, 1, 3, 0)
        for dh in (1, 0)
        for dl in (0, 1)
        if dy or dh or dl
    ]
    return column, plane


GROUP = 15


def spans():
    return [(c, tile * 8, tiles * 8) for c, (tile, tiles) in enumerate(CHUNKS)]


def split_dot(x, table):
    high = x.astype(BF16)
    rest = x - high.astype(F32)
    middle = rest.astype(BF16)
    low = (rest - middle.astype(F32)).astype(BF16)
    one = jnp.dot(low, table, preferred_element_type=F32)
    two = jnp.dot(middle, table, preferred_element_type=F32)
    return (one + two) + jnp.dot(high, table, preferred_element_type=F32)


def kernel(
    tv_hbm, k_hbm, r, gram_early, gram_late, total_ref, expand_ref,
    tv, kc, hz, f, fz, wn, prod, sum_early, sum_late,
    mine_early, mine_late, from_early, from_late,
    ysend, yrecv, fysend, fyrecv, edges, esend, erecv, ends, from_ends, sum_send, sum_recv,
    load_sem, a_send, a_recv, b_send, b_recv, pair_send, pair_recv, s_send, s_recv,
):
    gz, gy = lax.axis_index("gz"), lax.axis_index("gy")
    z_dev = (
        (lax.rem(gz + N_GZ - 1, N_GZ), gy),
        (lax.rem(gz + 1, N_GZ), gy),
    )
    y_dev = (
        (gz, lax.rem(gy + N_GY - 1, N_GY)),
        (gz, lax.rem(gy + 1, N_GY)),
    )
    partners = sum_partners()

    def remote(src, dst, send_sem, recv_sem, to):
        return pltpu.make_async_remote_copy(
            src_ref=src, dst_ref=dst, send_sem=send_sem, recv_sem=recv_sem,
            device_id=to, device_id_type=MESH,
        )

    def wait(sem, whole):
        pltpu.make_async_copy(whole, whole, sem).wait()

    def swap(at, sources, landing, to):
        for side in range(2):
            remote(
                sources.at[side], landing.at[1 - side], pair_send.at[at], pair_recv.at[at], to[side]
            ).start()

    loads = [
        pltpu.make_async_copy(tv_hbm, tv.at[:, :, pl.ds(PAD, ROWS), :], load_sem.at[0]),
        pltpu.make_async_copy(k_hbm, kc.at[:, pl.ds(PAD, ROWS), :], load_sem.at[1]),
    ]
    for copy in loads:
        copy.start()

    barrier = pltpu.get_barrier_semaphore()
    greeted = list(z_dev) + list(y_dev) + [d for group in partners for d in group]
    for to in greeted:
        pl.semaphore_signal(barrier, inc=1, device_id=to, device_id_type=MESH)

    pl.semaphore_wait(barrier, len(greeted))

    face = (0, 3)

    def send_faces(c, start, count):
        rows = pl.ds(start, count)
        for side in range(2):
            remote(
                k_hbm.at[face[side], rows, :], hz.at[1 - side, 4, rows, :],
                a_send.at[c], a_recv.at[c], z_dev[side],
            ).start()
            remote(
                tv_hbm.at[:, face[side], rows, :], hz.at[1 - side, pl.ds(0, 4), rows, :],
                a_send.at[c], a_recv.at[c], z_dev[side],
            ).start()

    send_faces(*spans()[0])
    for copy in loads:
        copy.wait()
    for side, row in ((0, PAD), (1, PAD + ROWS - 1)):
        for p in range(4):
            for v in range(4):
                ysend[side, pl.ds(v * 4 + p, 1), :] = tv[v, p, pl.ds(row, 1), :]
            ysend[side, pl.ds(16 + p, 1), :] = kc[p, pl.ds(row, 1), :]
        ysend[side, pl.ds(20, 4), :] = jnp.zeros((4, ACROSS), F32)
    swap(0, ysend, yrecv, y_dev)
    for span in spans()[1:]:
        send_faces(*span)

    for field in range(20):
        for side in range(2):
            prod[field, side, pl.ds(ROWS, 8), :] = jnp.zeros((8, 128), F32)
    for half in range(2):
        edges[half, 1] = jnp.zeros((8, 128), F32)
        for part in range(2):
            sum_early[half, part, pl.ds(80, 8), :] = jnp.zeros((8, ACROSS), F32)
    across = lax.broadcasted_iota(jnp.int32, (256, 2 * ACROSS), 1)
    owner = (((across + (ACROSS - 2)) & (ACROSS - 1)) >> 2) + ((across >> 8) << 6)
    source = lax.broadcasted_iota(jnp.int32, (256, 2 * ACROSS), 0) & 127
    expand_ref[...] = (source == owner).astype(F32).astype(BF16)

    wait(pair_recv.at[0], yrecv)
    for side, row in ((0, PAD - 1), (1, PAD + ROWS)):
        for p in range(4):
            for v in range(4):
                tv[v, p, pl.ds(row, 1), :] = yrecv[side, pl.ds(v * 4 + p, 1), :]
            kc[p, pl.ds(row, 1), :] = yrecv[side, pl.ds(16 + p, 1), :]

    def left(x):
        return pltpu.roll(x, 1, 1)

    def right(x):
        return pltpu.roll(x, ACROSS - 1, 1)

    def weights(t, p):
        at = t * 8
        here = kc[p, pl.ds(at + PAD, 8), :]
        near = (
            kc[p + 1, pl.ds(at + PAD, 8), :] if p < 3 else hz[1, 4, pl.ds(at, 8), :],
            kc[p - 1, pl.ds(at + PAD, 8), :] if p > 0 else hz[0, 4, pl.ds(at, 8), :],
            kc[p, pl.ds(at + PAD + 1, 8), :],
            kc[p, pl.ds(at + PAD - 1, 8), :],
            right(here),
            left(here),
        )
        parts = [n / (here + n) for n in near]
        total = ((parts[0] + parts[1]) + (parts[2] + parts[3])) + (parts[4] + parts[5])
        norm = STEP / total
        for i in range(6):
            wn[i, p, pl.ds(at, 8), :] = parts[i] * norm

    def relax(t, p, src, halo=None):
        at = t * 8
        w = [wn[i, p, pl.ds(at, 8), :] for i in range(6)]
        result = []
        for v in range(4):
            here = src[v, p, pl.ds(at + PAD, 8), :]
            up = src[v, p + 1, pl.ds(at + PAD, 8), :] if p < 3 else None
            down = src[v, p - 1, pl.ds(at + PAD, 8), :] if p > 0 else None
            if halo is not None and p == 3:
                up = halo[1, v, pl.ds(at, 8), :]
            if halo is not None and p == 0:
                down = halo[0, v, pl.ds(at, 8), :]
            ahead = src[v, p, pl.ds(at + PAD + 1, 8), :]
            behind = src[v, p, pl.ds(at + PAD - 1, 8), :]
            total = w[2] * ahead + w[3] * behind
            total = total + (w[4] * right(here) + w[5] * left(here))
            total = here * KEEP + total
            if up is not None:
                total = total + w[0] * up
            if down is not None:
                total = total + w[1] * down
            result.append(total)
        return result

    def first_tile(t, p):
        for v, value in enumerate(relax(t, p, tv, hz)):
            f[v, p, pl.ds(t * 8 + PAD, 8), :] = value

    def second_tile(t, p):
        for v, value in enumerate(relax(t, p, f)):
            r[v, p, pl.ds(t * 8, 8), :] = value

    def add_halo(t, half):
        rows = pl.ds(t * 8, 8)
        p = face[half]
        w = wn[1 - half, p, rows, :]
        for v in range(4):
            r[v, p, rows, :] = r[v, p, rows, :] + w * fz[half, v, rows, :]

    for t in range(TILES):
        for p in (1, 2):
            weights(t, p)
            first_tile(t, p)

    for c, start, count in spans():
        rows = pl.ds(start, count)
        wait(a_recv.at[c], hz.at[:, :, rows, :])
        for t in range(start // 8, (start + count) // 8):
            for p in face:
                weights(t, p)
                first_tile(t, p)
        for side in range(2):
            remote(
                f.at[:, face[side], pl.ds(start + PAD, count), :], fz.at[1 - side, :, rows, :],
                b_send.at[c], b_recv.at[c], z_dev[side],
            ).start()
        if c == 1:
            for side, row in ((0, PAD), (1, PAD + ROWS - 1)):
                for p in range(4):
                    for v in range(4):
                        fysend[side, pl.ds(v * 4 + p, 1), :] = f[v, p, pl.ds(row, 1), :]
            swap(1, fysend, fyrecv, y_dev)

    wait(pair_recv.at[1], fyrecv)
    for side, row in ((0, PAD - 1), (1, PAD + ROWS)):
        for p in range(4):
            for v in range(4):
                f[v, p, pl.ds(row, 1), :] = fyrecv[side, pl.ds(v * 4 + p, 1), :]
    for t in range(TILES):
        for p in range(4):
            second_tile(t, p)
    wait(pair_send.at[0], ysend)
    wait(pair_send.at[1], fysend)
    for c, start, count in spans():
        wait(a_send.at[c], hz.at[:, :, pl.ds(start, count), :])

    def group_sums(field, first_row, into, at):
        for side in range(2):
            parts = [prod[field, side, pl.ds(first_row + i, 8, stride=4), :] for i in range(4)]
            into[field // 10, (field % 10) // 5, pl.ds(at, 8), pl.ds(side * 128, 128)] = (
                (parts[0] + parts[1]) + (parts[2] + parts[3])
            )

    cell = ((lax.broadcasted_iota(jnp.int32, (ACROSS, 128), 0) + (ACROSS - 2)) & (ACROSS - 1)) >> 2
    lane = lax.broadcasted_iota(jnp.int32, (ACROSS, 128), 1)
    pick = [(cell + 64 * part == lane).astype(F32).astype(BF16) for part in range(2)]

    def pack(sums, half):
        return split_dot(sums[half, 0], pick[0]) + split_dot(sums[half, 1], pick[1])

    squares = [jnp.zeros((8, ACROSS), F32) for _ in range(4)]
    for c, start, count in spans():
        if c == len(CHUNKS) - 1:
            for field in range(20):
                n = field % 5
                group_sums(field, 2, sum_early, n * 8)
                group_sums(field, 66, sum_early, 40 + n * 8)
                for side in range(2):
                    sum_early[field // 10, (field % 10) // 5, pl.ds(80 + n, 1), pl.ds(side * 128, 128)] = (
                        prod[field, side, pl.ds(0, 1), :] + prod[field, side, pl.ds(1, 1), :]
                    )
            for half in range(2):
                packed = pack(sum_early, half)
                mine_early[half] = packed[:80]
                edges[half, 0] = packed[80:]
                for i in range(5):
                    edges[half, 1, pl.ds(i, 1), :] = packed[47 + 8 * i : 48 + 8 * i]
            swap(2, mine_early, from_early, z_dev)
            for half in range(2):
                esend[0, half] = edges[half, 0]
                esend[1, half] = edges[half, 1]
            swap(4, esend, erecv, y_dev)
        wait(b_recv.at[c], fz.at[:, :, pl.ds(start, count), :])
        for t in range(start // 8, (start + count) // 8):
            rows = pl.ds(t * 8, 8)
            for half in range(2):
                add_halo(t, half)
                low = [r[v, 2 * half, rows, :] for v in range(4)]
                high = [r[v, 2 * half + 1, rows, :] for v in range(4)]
                for i, (a, b) in enumerate(PAIRS):
                    value = low[a] * low[b] + high[a] * high[b]
                    prod[half * 10 + i, 0, rows, :] = value[:, :128]
                    prod[half * 10 + i, 1, rows, :] = value[:, 128:]
                    if a == b:
                        squares[a] = squares[a] + value

    def exchange(stage):
        for i, to in enumerate(partners[stage]):
            remote(
                sum_send.at[stage], sum_recv.at[stage, i], s_send.at[stage], s_recv.at[stage], to
            ).start()

    def collect(stage):
        wait(s_recv.at[stage], sum_recv.at[stage])
        total = [sum_send[stage]] + [sum_recv[stage, i] for i in range(GROUP)]
        while len(total) > 1:
            total = [total[i] + total[i + 1] for i in range(0, len(total), 2)]
        return total[0]

    stacked = [jnp.sum(q[:, :128] + q[:, 128:], axis=0, keepdims=True) for q in squares]
    stacked = jnp.concatenate(stacked + [jnp.zeros((4, 128), F32)], axis=0)
    stacked = jnp.sum(stacked, axis=1, keepdims=True)
    on_diagonal = lax.broadcasted_iota(jnp.int32, (8, 128), 0) == lax.broadcasted_iota(
        jnp.int32, (8, 128), 1
    )
    sum_send[0] = jnp.sum(jnp.where(on_diagonal, stacked, 0.0), axis=0, keepdims=True)
    exchange(0)

    for field in range(20):
        group_sums(field, 34, sum_late, (field % 5) * 8)
    for half in range(2):
        mine_late[half] = pack(sum_late, half)
    swap(3, mine_late, from_late, z_dev)
    wait(pair_recv.at[4], erecv)
    for half in range(2):
        for kind in range(2):
            ends[half, kind] = edges[half, kind] + erecv[kind, half]
    swap(5, ends, from_ends, z_dev)
    for c, start, count in spans():
        wait(b_send.at[c], fz.at[:, :, pl.ds(start, count), :])

    sum_send[1] = collect(0)
    exchange(1)

    wait(pair_recv.at[2], from_early)
    for half in range(2):
        gram_early[half, pl.ds(0, 80), :] = mine_early[half] + from_early[half]
    wait(pair_recv.at[3], from_late)
    for half in range(2):
        gram_late[half] = mine_late[half] + from_late[half]
    wait(pair_recv.at[5], from_ends)
    for half in range(2):
        gram_early[half, pl.ds(80, 8), :] = ends[half, 0] + from_ends[half, 0]
        last = ends[half, 1] + from_ends[half, 1]
        for i in range(5):
            gram_early[half, pl.ds(47 + 8 * i, 1), :] = last[i : i + 1]
    wait(pair_send.at[2], mine_early)
    wait(pair_send.at[3], mine_late)
    wait(pair_send.at[4], esend)
    wait(pair_send.at[5], ends)
    wait(s_send.at[0], sum_recv.at[0])
    total_ref[...] = jnp.broadcast_to(collect(1), (8, 128))
    wait(s_send.at[1], sum_recv.at[1])


def finish(
    r, gram_early, gram_late, total_ref, expand, out_hbm, fac_hbm, spread, out, fac, out_sem, fac_sem
):
    is_low = lax.broadcasted_iota(jnp.int32, (32, 128), 1) < 64
    lane = lax.broadcasted_iota(jnp.int32, (1, 128), 1)
    scale_row = lax.rsqrt(total_ref[0:1, :] / CELLS + 1e-06)
    scale = [
        jnp.sum(jnp.where(lane == v, scale_row, 0.0), axis=1, keepdims=True) for v in range(4)
    ]

    def groups(half, i):
        edge = jnp.broadcast_to(gram_early[half, pl.ds(80 + i, 1), :], (8, 128))
        return jnp.concatenate(
            [
                edge,
                gram_early[half, pl.ds(8 * i, 8), :],
                gram_late[half, pl.ds(8 * i, 8), :],
                gram_early[half, pl.ds(40 + 8 * i, 8), :],
            ],
            axis=0,
        )

    gram = [None] * 10
    for i in range(5):
        low, high = groups(0, i), groups(1, i)
        gram[i] = jnp.where(is_low, low, pltpu.roll(high, 64, 1))
        gram[i + 5] = jnp.where(is_low, pltpu.roll(low, 64, 1), high)

    m = {pair: gram[i] * (scale[pair[0]] * scale[pair[1]]) for i, pair in enumerate(PAIRS)}
    trace = (m[0, 0] + m[1, 1]) + (m[2, 2] + m[3, 3])
    ridge = 0.64 * (trace / 256.0 + 1e-06)
    upper, inverse = {}, []
    for i in range(4):
        for j in range(i, 4):
            value = m[i, j]
            if i == j:
                value = value + ridge
            for n in range(i):
                value = value - upper[n, i] * upper[n, j]
            if i == j:
                upper[i, i] = jnp.sqrt(value)
                inverse.append(1.0 / upper[i, i])
            else:
                upper[i, j] = value * inverse[i]
    table = [(scale[j] if i == j else upper[i, j]) * inverse[j] for i, j in PAIRS]
    table = jnp.concatenate(table, axis=0)
    high = table.astype(BF16)
    rest = table - high.astype(F32)
    middle = rest.astype(BF16)
    low = (rest - middle.astype(F32)).astype(BF16)
    wide = jnp.dot(low, expand[pl.ds(0, 128), :], preferred_element_type=F32) + jnp.dot(
        jnp.concatenate([high, middle], axis=1), expand[...], preferred_element_type=F32
    )
    spread[...] = wide.reshape(10, 32, 2 * ACROSS)
    for n, pair in enumerate(PAIRS):
        fac[n, 0] = pltpu.roll(upper[pair], 64, 1)[8:32, :64]
    fac_copy = pltpu.make_async_copy(fac, fac_hbm, fac_sem)
    fac_copy.start()

    sub = lax.broadcasted_iota(jnp.int32, (8, ACROSS), 0)
    before, after = sub < 2, sub >= 6

    def store(c):
        rows = pl.ds(pl.multiple_of(c * 24, 8), 24)
        return pltpu.make_async_copy(out.at[:, :, rows, :], out_hbm.at[:, :, rows, :], out_sem.at[c])

    @pl.loop(0, 4)
    def _(c):
        for n_tile in range(3):
            t = c * 3 + n_tile
            rows = pl.ds(pl.multiple_of(t * 8, 8), 8)
            for half in range(2):
                columns = pl.ds(half * ACROSS, ACROSS)
                field = []
                for n in range(10):
                    one, two, three = [spread[n, pl.ds(2 * t + 7 + i, 1), columns] for i in range(3)]
                    field.append(jnp.where(before, one, jnp.where(after, three, two)))
                for p in (2 * half, 2 * half + 1):
                    done_columns = []
                    for j in range(4):
                        value = r[j, p, rows, :] * field[AT[j, j]]
                        for i in range(j):
                            value = value - field[AT[i, j]] * done_columns[i]
                        done_columns.append(value)
                        out[j, p, rows, :] = value
        store(c).start()

    fac_copy.wait()
    for c in range(4):
        store(c).wait()


def body(test_vectors, conductivity):
    vm = lambda *shape: pltpu.VMEM(shape, F32)
    dma = lambda *shape: pltpu.SemaphoreType.DMA(shape)
    shape = lambda *dims: jax.ShapeDtypeStruct(dims, F32)
    in_vmem = pl.BlockSpec(memory_space=pltpu.VMEM)
    anywhere = pl.BlockSpec(memory_space=pl.ANY)
    n = len(CHUNKS)
    padded = ROWS + 2 * PAD
    staged = pl.pallas_call(
        kernel,
        out_shape=(
            shape(4, 4, ROWS, ACROSS),
            shape(2, EARLY, 128),
            shape(2, LATE, 128),
            shape(8, 128),
            jax.ShapeDtypeStruct((256, 2 * ACROSS), BF16),
        ),
        in_specs=[pl.BlockSpec(memory_space=pltpu.HBM)] * 2,
        out_specs=(in_vmem,) * 5,
        scratch_shapes=[
            vm(4, 4, padded, ACROSS),
            vm(4, padded, ACROSS),
            vm(2, 5, ROWS, ACROSS),
            vm(4, 4, padded, ACROSS),
            vm(2, 4, ROWS, ACROSS),
            vm(6, 4, ROWS, ACROSS),
            vm(20, 2, ROWS + 8, 128),
            vm(2, 2, EARLY, ACROSS),
            vm(2, 2, LATE, ACROSS),
            vm(2, EARLY - 8, 128),
            vm(2, LATE, 128),
            vm(2, EARLY - 8, 128),
            vm(2, LATE, 128),
            vm(2, 24, ACROSS),
            vm(2, 24, ACROSS),
            vm(2, 16, ACROSS),
            vm(2, 16, ACROSS),
            vm(2, 2, 8, 128),
            vm(2, 2, 8, 128),
            vm(2, 2, 8, 128),
            vm(2, 2, 8, 128),
            vm(2, 2, 8, 128),
            vm(2, 1, 128),
            vm(2, GROUP, 1, 128),
            dma(2),
            dma(n), dma(n), dma(n), dma(n), dma(6), dma(6), dma(2), dma(2),
        ],
        compiler_params=pltpu.CompilerParams(
            collective_id=0, has_side_effects=True, vmem_limit_bytes=24 << 20
        ),
        name="relax",
    )(*[pltpu.with_memory_space_constraint(x, pltpu.HBM) for x in (test_vectors, conductivity)])
    return pl.pallas_call(
        finish,
        out_shape=(shape(4, 4, ROWS, ACROSS), shape(10, 1, 24, 64)),
        in_specs=[in_vmem] * 5,
        out_specs=(anywhere, anywhere),
        scratch_shapes=[
            vm(10, 32, 2 * ACROSS),
            vm(4, 4, ROWS, ACROSS),
            vm(10, 1, 24, 64),
            dma(4),
            pltpu.SemaphoreType.DMA,
        ],
        compiler_params=pltpu.CompilerParams(vmem_limit_bytes=16 << 20),
        name="finish",
    )(*staged)


def solution(mesh):
    return jax.shard_map(
        body,
        mesh=mesh,
        in_specs=(P(None, "gz", "gy", None), P("gz", "gy", None)),
        out_specs=(P(None, "gz", "gy", None), P(None, "gz", "gy", None)),
        check_vma=False,
    )
```

```python
import functools

import jax
import jax.numpy as jnp
from jax import lax
from jax.experimental import pallas as pl
from jax.experimental.pallas import tpu as pltpu
from jax.sharding import PartitionSpec as P

MESH = pl.DeviceIdType.MESH
F32 = jnp.float32
KEEP = 1.0 / 3.0
STEP = 2.0 / 3.0
PAIRS = ((0, 0), (0, 1), (0, 2), (0, 3), (1, 1), (1, 2), (1, 3), (2, 2), (2, 3), (3, 3))
AT = {pair: i for i, pair in enumerate(PAIRS)}
BF16 = jnp.bfloat16
ROWS = 96
ACROSS = 256
PAD = 8
TILES = ROWS // 8
CHUNKS = ((0, 2), (10, 2), (8, 2), (2, 3), (5, 2), (7, 1))
EARLY = 88
LATE = 40
N_GZ = 64
N_GY = 4
CELLS = 256 * 384 * 256


def device(z, y, x_hi, x_lo, core):
    return (z * 8 + y * 2 + x_hi, x_lo * 2 + core)


def sum_partners():
    gz, gy = lax.axis_index("gz"), lax.axis_index("gy")
    z, y, x_hi = gz // 8, lax.rem(gz, 8) // 2, lax.rem(gz, 2)
    x_lo, core = gy // 2, lax.rem(gy, 2)
    column = [
        device(lax.rem(z + dz, 8), y, x_hi, x_lo, lax.rem(core + dc, 2))
        for dz in (4, 3, 5, 2, 6, 1, 7, 0)
        for dc in (1, 0)
        if dz or dc
    ]
    plane = [
        device(z, lax.rem(y + dy, 4), lax.rem(x_hi + dh, 2), lax.rem(x_lo + dl, 2), core)
        for dy in (2, 1, 3, 0)
        for dh in (1, 0)
        for dl in (0, 1)
        if dy or dh or dl
    ]
    return column, plane


GROUP = 15


def spans():
    return [(c, tile * 8, tiles * 8) for c, (tile, tiles) in enumerate(CHUNKS)]


def split_dot(x, table):
    high = x.astype(BF16)
    rest = x - high.astype(F32)
    middle = rest.astype(BF16)
    low = (rest - middle.astype(F32)).astype(BF16)
    one = jnp.dot(low, table, preferred_element_type=F32)
    two = jnp.dot(middle, table, preferred_element_type=F32)
    return (one + two) + jnp.dot(high, table, preferred_element_type=F32)


def kernel(
    tv_hbm, k_hbm, r, gram_early, gram_late, total_ref, expand_ref,
    tv, kc, hz, f, fz, wn, prod, sum_early, sum_late,
    mine_early, mine_late, from_early, from_late,
    ysend, yrecv, fysend, fyrecv, edges, esend, erecv, ends, from_ends, sum_send, sum_recv,
    load_sem, a_send, a_recv, b_send, b_recv, pair_send, pair_recv, s_send, s_recv,
):
    gz, gy = lax.axis_index("gz"), lax.axis_index("gy")
    z_dev = (
        (lax.rem(gz + N_GZ - 1, N_GZ), gy),
        (lax.rem(gz + 1, N_GZ), gy),
    )
    y_dev = (
        (gz, lax.rem(gy + N_GY - 1, N_GY)),
        (gz, lax.rem(gy + 1, N_GY)),
    )
    partners = sum_partners()

    def remote(src, dst, send_sem, recv_sem, to):
        return pltpu.make_async_remote_copy(
            src_ref=src, dst_ref=dst, send_sem=send_sem, recv_sem=recv_sem,
            device_id=to, device_id_type=MESH,
        )

    def wait(sem, whole):
        pltpu.make_async_copy(whole, whole, sem).wait()

    def swap(at, sources, landing, to):
        for side in range(2):
            remote(
                sources.at[side], landing.at[1 - side], pair_send.at[at], pair_recv.at[at], to[side]
            ).start()

    loads = [
        pltpu.make_async_copy(tv_hbm, tv.at[:, :, pl.ds(PAD, ROWS), :], load_sem.at[0]),
        pltpu.make_async_copy(k_hbm, kc.at[:, pl.ds(PAD, ROWS), :], load_sem.at[1]),
    ]
    for copy in loads:
        copy.start()

    barrier = pltpu.get_barrier_semaphore()
    greeted = list(z_dev) + list(y_dev) + [d for group in partners for d in group]
    for to in greeted:
        pl.semaphore_signal(barrier, inc=1, device_id=to, device_id_type=MESH)

    pl.semaphore_wait(barrier, len(greeted))

    face = (0, 3)

    def send_faces(c, start, count):
        rows = pl.ds(start, count)
        for side in range(2):
            remote(
                k_hbm.at[face[side], rows, :], hz.at[1 - side, 4, rows, :],
                a_send.at[c], a_recv.at[c], z_dev[side],
            ).start()
            remote(
                tv_hbm.at[:, face[side], rows, :], hz.at[1 - side, pl.ds(0, 4), rows, :],
                a_send.at[c], a_recv.at[c], z_dev[side],
            ).start()

    send_faces(*spans()[0])
    for copy in loads:
        copy.wait()
    for side, row in ((0, PAD), (1, PAD + ROWS - 1)):
        for p in range(4):
            for v in range(4):
                ysend[side, pl.ds(v * 4 + p, 1), :] = tv[v, p, pl.ds(row, 1), :]
            ysend[side, pl.ds(16 + p, 1), :] = kc[p, pl.ds(row, 1), :]
        ysend[side, pl.ds(20, 4), :] = jnp.zeros((4, ACROSS), F32)
    swap(0, ysend, yrecv, y_dev)
    for span in spans()[1:]:
        send_faces(*span)

    for field in range(20):
        for side in range(2):
            prod[field, side, pl.ds(ROWS, 8), :] = jnp.zeros((8, 128), F32)
    for half in range(2):
        edges[half, 1] = jnp.zeros((8, 128), F32)
        for part in range(2):
            sum_early[half, part, pl.ds(80, 8), :] = jnp.zeros((8, ACROSS), F32)
    across = lax.broadcasted_iota(jnp.int32, (256, 2 * ACROSS), 1)
    owner = (((across + (ACROSS - 2)) & (ACROSS - 1)) >> 2) + ((across >> 8) << 6)
    source = lax.broadcasted_iota(jnp.int32, (256, 2 * ACROSS), 0) & 127
    expand_ref[...] = (source == owner).astype(F32).astype(BF16)

    wait(pair_recv.at[0], yrecv)
    for side, row in ((0, PAD - 1), (1, PAD + ROWS)):
        for p in range(4):
            for v in range(4):
                tv[v, p, pl.ds(row, 1), :] = yrecv[side, pl.ds(v * 4 + p, 1), :]
            kc[p, pl.ds(row, 1), :] = yrecv[side, pl.ds(16 + p, 1), :]

    def left(x):
        return pltpu.roll(x, 1, 1)

    def right(x):
        return pltpu.roll(x, ACROSS - 1, 1)

    def weights(t, p):
        at = t * 8
        here = kc[p, pl.ds(at + PAD, 8), :]
        near = (
            kc[p + 1, pl.ds(at + PAD, 8), :] if p < 3 else hz[1, 4, pl.ds(at, 8), :],
            kc[p - 1, pl.ds(at + PAD, 8), :] if p > 0 else hz[0, 4, pl.ds(at, 8), :],
            kc[p, pl.ds(at + PAD + 1, 8), :],
            kc[p, pl.ds(at + PAD - 1, 8), :],
            right(here),
            left(here),
        )
        parts = [n / (here + n) for n in near]
        total = ((parts[0] + parts[1]) + (parts[2] + parts[3])) + (parts[4] + parts[5])
        norm = STEP / total
        for i in range(6):
            wn[i, p, pl.ds(at, 8), :] = parts[i] * norm

    def relax(t, p, src, halo=None):
        at = t * 8
        w = [wn[i, p, pl.ds(at, 8), :] for i in range(6)]
        result = []
        for v in range(4):
            here = src[v, p, pl.ds(at + PAD, 8), :]
            up = src[v, p + 1, pl.ds(at + PAD, 8), :] if p < 3 else None
            down = src[v, p - 1, pl.ds(at + PAD, 8), :] if p > 0 else None
            if halo is not None and p == 3:
                up = halo[1, v, pl.ds(at, 8), :]
            if halo is not None and p == 0:
                down = halo[0, v, pl.ds(at, 8), :]
            ahead = src[v, p, pl.ds(at + PAD + 1, 8), :]
            behind = src[v, p, pl.ds(at + PAD - 1, 8), :]
            total = w[2] * ahead + w[3] * behind
            total = total + (w[4] * right(here) + w[5] * left(here))
            total = here * KEEP + total
            if up is not None:
                total = total + w[0] * up
            if down is not None:
                total = total + w[1] * down
            result.append(total)
        return result

    def first_tile(t, p):
        for v, value in enumerate(relax(t, p, tv, hz)):
            f[v, p, pl.ds(t * 8 + PAD, 8), :] = value

    def second_tile(t, p):
        for v, value in enumerate(relax(t, p, f)):
            r[v, p, pl.ds(t * 8, 8), :] = value

    def add_halo(t, half):
        rows = pl.ds(t * 8, 8)
        p = face[half]
        w = wn[1 - half, p, rows, :]
        for v in range(4):
            r[v, p, rows, :] = r[v, p, rows, :] + w * fz[half, v, rows, :]

    for t in range(TILES):
        for p in (1, 2):
            weights(t, p)
            first_tile(t, p)

    for c, start, count in spans():
        rows = pl.ds(start, count)
        wait(a_recv.at[c], hz.at[:, :, rows, :])
        for t in range(start // 8, (start + count) // 8):
            for p in face:
                weights(t, p)
                first_tile(t, p)
        for side in range(2):
            remote(
                f.at[:, face[side], pl.ds(start + PAD, count), :], fz.at[1 - side, :, rows, :],
                b_send.at[c], b_recv.at[c], z_dev[side],
            ).start()
        if c == 1:
            for side, row in ((0, PAD), (1, PAD + ROWS - 1)):
                for p in range(4):
                    for v in range(4):
                        fysend[side, pl.ds(v * 4 + p, 1), :] = f[v, p, pl.ds(row, 1), :]
            swap(1, fysend, fyrecv, y_dev)

    wait(pair_recv.at[1], fyrecv)
    for side, row in ((0, PAD - 1), (1, PAD + ROWS)):
        for p in range(4):
            for v in range(4):
                f[v, p, pl.ds(row, 1), :] = fyrecv[side, pl.ds(v * 4 + p, 1), :]
    for t in range(TILES):
        for p in range(4):
            second_tile(t, p)
    wait(pair_send.at[0], ysend)
    wait(pair_send.at[1], fysend)
    for c, start, count in spans():
        wait(a_send.at[c], hz.at[:, :, pl.ds(start, count), :])

    def group_sums(field, first_row, into, at):
        for side in range(2):
            parts = [prod[field, side, pl.ds(first_row + i, 8, stride=4), :] for i in range(4)]
            into[field // 10, (field % 10) // 5, pl.ds(at, 8), pl.ds(side * 128, 128)] = (
                (parts[0] + parts[1]) + (parts[2] + parts[3])
            )

    cell = ((lax.broadcasted_iota(jnp.int32, (ACROSS, 128), 0) + (ACROSS - 2)) & (ACROSS - 1)) >> 2
    lane = lax.broadcasted_iota(jnp.int32, (ACROSS, 128), 1)
    pick = [(cell + 64 * part == lane).astype(F32).astype(BF16) for part in range(2)]

    def pack(sums, half):
        return split_dot(sums[half, 0], pick[0]) + split_dot(sums[half, 1], pick[1])

    squares = [jnp.zeros((8, ACROSS), F32) for _ in range(4)]
    for c, start, count in spans():
        if c == len(CHUNKS) - 1:
            for field in range(20):
                n = field % 5
                group_sums(field, 2, sum_early, n * 8)
                group_sums(field, 66, sum_early, 40 + n * 8)
                for side in range(2):
                    sum_early[field // 10, (field % 10) // 5, pl.ds(80 + n, 1), pl.ds(side * 128, 128)] = (
                        prod[field, side, pl.ds(0, 1), :] + prod[field, side, pl.ds(1, 1), :]
                    )
            for half in range(2):
                packed = pack(sum_early, half)
                mine_early[half] = packed[:80]
                edges[half, 0] = packed[80:]
                for i in range(5):
                    edges[half, 1, pl.ds(i, 1), :] = packed[47 + 8 * i : 48 + 8 * i]
            for half in range(2):
                esend[0, half] = edges[half, 0]
                esend[1, half] = edges[half, 1]
            swap(4, esend, erecv, y_dev)
        wait(b_recv.at[c], fz.at[:, :, pl.ds(start, count), :])
        for t in range(start // 8, (start + count) // 8):
            rows = pl.ds(t * 8, 8)
            for half in range(2):
                add_halo(t, half)
                low = [r[v, 2 * half, rows, :] for v in range(4)]
                high = [r[v, 2 * half + 1, rows, :] for v in range(4)]
                for i, (a, b) in enumerate(PAIRS):
                    value = low[a] * low[b] + high[a] * high[b]
                    prod[half * 10 + i, 0, rows, :] = value[:, :128]
                    prod[half * 10 + i, 1, rows, :] = value[:, 128:]
                    if a == b:
                        squares[a] = squares[a] + value

    def exchange(stage):
        for i, to in enumerate(partners[stage]):
            remote(
                sum_send.at[stage], sum_recv.at[stage, i], s_send.at[stage], s_recv.at[stage], to
            ).start()

    def collect(stage):
        wait(s_recv.at[stage], sum_recv.at[stage])
        total = [sum_send[stage]] + [sum_recv[stage, i] for i in range(GROUP)]
        while len(total) > 1:
            total = [total[i] + total[i + 1] for i in range(0, len(total), 2)]
        return total[0]

    stacked = [jnp.sum(q[:, :128] + q[:, 128:], axis=0, keepdims=True) for q in squares]
    stacked = jnp.concatenate(stacked + [jnp.zeros((4, 128), F32)], axis=0)
    stacked = jnp.sum(stacked, axis=1, keepdims=True)
    on_diagonal = lax.broadcasted_iota(jnp.int32, (8, 128), 0) == lax.broadcasted_iota(
        jnp.int32, (8, 128), 1
    )
    sum_send[0] = jnp.sum(jnp.where(on_diagonal, stacked, 0.0), axis=0, keepdims=True)
    exchange(0)

    for field in range(20):
        group_sums(field, 34, sum_late, (field % 5) * 8)
    for half in range(2):
        mine_late[half] = pack(sum_late, half)
    swap(3, mine_late, from_late, z_dev)
    swap(2, mine_early, from_early, z_dev)
    wait(pair_recv.at[4], erecv)
    for half in range(2):
        for kind in range(2):
            ends[half, kind] = edges[half, kind] + erecv[kind, half]
    swap(5, ends, from_ends, z_dev)
    for c, start, count in spans():
        wait(b_send.at[c], fz.at[:, :, pl.ds(start, count), :])

    sum_send[1] = collect(0)
    exchange(1)

    wait(pair_recv.at[2], from_early)
    for half in range(2):
        gram_early[half, pl.ds(0, 80), :] = mine_early[half] + from_early[half]
    wait(pair_recv.at[3], from_late)
    for half in range(2):
        gram_late[half] = mine_late[half] + from_late[half]
    wait(pair_recv.at[5], from_ends)
    for half in range(2):
        gram_early[half, pl.ds(80, 8), :] = ends[half, 0] + from_ends[half, 0]
        last = ends[half, 1] + from_ends[half, 1]
        for i in range(5):
            gram_early[half, pl.ds(47 + 8 * i, 1), :] = last[i : i + 1]
    wait(pair_send.at[2], mine_early)
    wait(pair_send.at[3], mine_late)
    wait(pair_send.at[4], esend)
    wait(pair_send.at[5], ends)
    wait(s_send.at[0], sum_recv.at[0])
    total_ref[...] = jnp.broadcast_to(collect(1), (8, 128))
    wait(s_send.at[1], sum_recv.at[1])


def finish(
    r, gram_early, gram_late, total_ref, expand, out_hbm, fac_hbm, spread, out, fac, out_sem, fac_sem
):
    is_low = lax.broadcasted_iota(jnp.int32, (32, 128), 1) < 64
    lane = lax.broadcasted_iota(jnp.int32, (1, 128), 1)
    scale_row = lax.rsqrt(total_ref[0:1, :] / CELLS + 1e-06)
    scale = [
        jnp.sum(jnp.where(lane == v, scale_row, 0.0), axis=1, keepdims=True) for v in range(4)
    ]

    def groups(half, i):
        edge = jnp.broadcast_to(gram_early[half, pl.ds(80 + i, 1), :], (8, 128))
        return jnp.concatenate(
            [
                edge,
                gram_early[half, pl.ds(8 * i, 8), :],
                gram_late[half, pl.ds(8 * i, 8), :],
                gram_early[half, pl.ds(40 + 8 * i, 8), :],
            ],
            axis=0,
        )

    gram = [None] * 10
    for i in range(5):
        low, high = groups(0, i), groups(1, i)
        gram[i] = jnp.where(is_low, low, pltpu.roll(high, 64, 1))
        gram[i + 5] = jnp.where(is_low, pltpu.roll(low, 64, 1), high)

    m = {pair: gram[i] * (scale[pair[0]] * scale[pair[1]]) for i, pair in enumerate(PAIRS)}
    trace = (m[0, 0] + m[1, 1]) + (m[2, 2] + m[3, 3])
    ridge = 0.64 * (trace / 256.0 + 1e-06)
    upper, inverse = {}, []
    for i in range(4):
        for j in range(i, 4):
            value = m[i, j]
            if i == j:
                value = value + ridge
            for n in range(i):
                value = value - upper[n, i] * upper[n, j]
            if i == j:
                upper[i, i] = jnp.sqrt(value)
                inverse.append(1.0 / upper[i, i])
            else:
                upper[i, j] = value * inverse[i]
    table = [(scale[j] if i == j else upper[i, j]) * inverse[j] for i, j in PAIRS]
    table = jnp.concatenate(table, axis=0)
    high = table.astype(BF16)
    rest = table - high.astype(F32)
    middle = rest.astype(BF16)
    low = (rest - middle.astype(F32)).astype(BF16)
    wide = jnp.dot(low, expand[pl.ds(0, 128), :], preferred_element_type=F32) + jnp.dot(
        jnp.concatenate([high, middle], axis=1), expand[...], preferred_element_type=F32
    )
    spread[...] = wide.reshape(10, 32, 2 * ACROSS)
    for n, pair in enumerate(PAIRS):
        fac[n, 0] = pltpu.roll(upper[pair], 64, 1)[8:32, :64]
    fac_copy = pltpu.make_async_copy(fac, fac_hbm, fac_sem)
    fac_copy.start()

    sub = lax.broadcasted_iota(jnp.int32, (8, ACROSS), 0)
    before, after = sub < 2, sub >= 6

    def store(c):
        rows = pl.ds(pl.multiple_of(c * 24, 8), 24)
        return pltpu.make_async_copy(out.at[:, :, rows, :], out_hbm.at[:, :, rows, :], out_sem.at[c])

    @pl.loop(0, 4)
    def _(c):
        for n_tile in range(3):
            t = c * 3 + n_tile
            rows = pl.ds(pl.multiple_of(t * 8, 8), 8)
            for half in range(2):
                columns = pl.ds(half * ACROSS, ACROSS)
                field = []
                for n in range(10):
                    one, two, three = [spread[n, pl.ds(2 * t + 7 + i, 1), columns] for i in range(3)]
                    field.append(jnp.where(before, one, jnp.where(after, three, two)))
                for p in (2 * half, 2 * half + 1):
                    done_columns = []
                    for j in range(4):
                        value = r[j, p, rows, :] * field[AT[j, j]]
                        for i in range(j):
                            value = value - field[AT[i, j]] * done_columns[i]
                        done_columns.append(value)
                        out[j, p, rows, :] = value
        store(c).start()

    fac_copy.wait()
    for c in range(4):
        store(c).wait()


def body(test_vectors, conductivity):
    vm = lambda *shape: pltpu.VMEM(shape, F32)
    dma = lambda *shape: pltpu.SemaphoreType.DMA(shape)
    shape = lambda *dims: jax.ShapeDtypeStruct(dims, F32)
    in_vmem = pl.BlockSpec(memory_space=pltpu.VMEM)
    anywhere = pl.BlockSpec(memory_space=pl.ANY)
    n = len(CHUNKS)
    padded = ROWS + 2 * PAD
    staged = pl.pallas_call(
        kernel,
        out_shape=(
            shape(4, 4, ROWS, ACROSS),
            shape(2, EARLY, 128),
            shape(2, LATE, 128),
            shape(8, 128),
            jax.ShapeDtypeStruct((256, 2 * ACROSS), BF16),
        ),
        in_specs=[pl.BlockSpec(memory_space=pltpu.HBM)] * 2,
        out_specs=(in_vmem,) * 5,
        scratch_shapes=[
            vm(4, 4, padded, ACROSS),
            vm(4, padded, ACROSS),
            vm(2, 5, ROWS, ACROSS),
            vm(4, 4, padded, ACROSS),
            vm(2, 4, ROWS, ACROSS),
            vm(6, 4, ROWS, ACROSS),
            vm(20, 2, ROWS + 8, 128),
            vm(2, 2, EARLY, ACROSS),
            vm(2, 2, LATE, ACROSS),
            vm(2, EARLY - 8, 128),
            vm(2, LATE, 128),
            vm(2, EARLY - 8, 128),
            vm(2, LATE, 128),
            vm(2, 24, ACROSS),
            vm(2, 24, ACROSS),
            vm(2, 16, ACROSS),
            vm(2, 16, ACROSS),
            vm(2, 2, 8, 128),
            vm(2, 2, 8, 128),
            vm(2, 2, 8, 128),
            vm(2, 2, 8, 128),
            vm(2, 2, 8, 128),
            vm(2, 1, 128),
            vm(2, GROUP, 1, 128),
            dma(2),
            dma(n), dma(n), dma(n), dma(n), dma(6), dma(6), dma(2), dma(2),
        ],
        compiler_params=pltpu.CompilerParams(
            collective_id=0, has_side_effects=True, vmem_limit_bytes=24 << 20
        ),
        name="relax",
    )(*[pltpu.with_memory_space_constraint(x, pltpu.HBM) for x in (test_vectors, conductivity)])
    return pl.pallas_call(
        finish,
        out_shape=(shape(4, 4, ROWS, ACROSS), shape(10, 1, 24, 64)),
        in_specs=[in_vmem] * 5,
        out_specs=(anywhere, anywhere),
        scratch_shapes=[
            vm(10, 32, 2 * ACROSS),
            vm(4, 4, ROWS, ACROSS),
            vm(10, 1, 24, 64),
            dma(4),
            pltpu.SemaphoreType.DMA,
        ],
        compiler_params=pltpu.CompilerParams(vmem_limit_bytes=16 << 20),
        name="finish",
    )(*staged)


def solution(mesh):
    return jax.shard_map(
        body,
        mesh=mesh,
        in_specs=(P(None, "gz", "gy", None), P("gz", "gy", None)),
        out_specs=(P(None, "gz", "gy", None), P(None, "gz", "gy", None)),
        check_vma=False,
    )
```
